256 devices in a mesh: req: 16 (over y_hi, x, core), tp: 16 (over y_lo, z).
Axes of the slice: x: 4, y: 4 (y_hi: 2, y_lo: 2; y = y_hi * 2 + y_lo), z: 8, core: 2. Of those that a mesh axis runs over, the one named last changes fastest.
Arguments:
- tokens: bfloat16 [14336, 5120], P(('req', 'tp')), may hold values from -6 to 6
- qkv_weight: bfloat16 [5120, 3, 4096], P('req', None, 'tp')
- out_weight: bfloat16 [4096, 5120], P('tp', 'req')
- query_key_gain: float32 [2, 4096], P(None, 'tp'), may hold values from 0.25 to 1.75
- post_gain: float32 [5120], replicated, may hold values from 0.25 to 1.75
- pool_cache: bfloat16 [512, 128, 2, 4096], P('req', None, None, 'tp'), may hold values from -68 to 68
- lengths: int32 [16, 16], P('req'), may hold values from 1 to 256, 896 in all within a row
- prefix_pages: int32 [16, 16], P('req'), may hold values from 1 to 16, 32 in all within a row
- pool_order: int32 [16, 32], P('req'), may hold values from 0 to 31, each once within a row
- owners: int32 [16, 16], P('req'), may hold values from 0 to 15, each once within a row
Outputs:
- hidden: bfloat16 [14336, 5120], P(('req', 'tp'))
- handed_pages: bfloat16 [512, 128, 2, 4096], P('req', None, None, 'tp')
The draws below stay inside these ranges and needn't reach their ends.
Inputs may be any that keep to these rules, and one draw needn't show every extreme that they name: `lengths`: each row sums to 896; the largest entry of every row is exactly 256. `prefix_pages`: each row sums to 32; the largest entry of every row is exactly 16. `pool_order`: each row names every slot once. `owners`: each row names every owner once.
All inputs are finite; a program needn't handle non-finite values.
Results may differ from the reference program's by a relative error of at most 0.014.
Values may be sent and summed in bfloat16 or wider, within the bound.
A program may use at most 128 MiB of HBM per device.

```python
import math
import jax
import jax.numpy as jnp
import numpy as np
from jax import lax

D = 5120
HEADS = 32
HEAD = 128
PAGE = 128
CAP = 2
BLOCK = 896
REQS = 16
POOL = 32
PMAX = 16
HD = 4096
TOKENS = 14336
N_REQ = 16
N_TP = 16


def draw_qkv_weight(key, part):
    normal_part = jnp.clip(jax.random.normal(key, (D, 3, HD), jnp.float32), -6.0, 6.0)
    head_index = (jnp.arange(HD) // HEAD).astype(jnp.float32)
    rising = 3.0 ** (head_index / max(HEADS - 1, 1))
    column_scale = jnp.stack([rising, rising, jnp.ones_like(rising)])
    return (normal_part * column_scale[None, :, :] / math.sqrt(D)).astype(jnp.bfloat16)


def draw_out_weight(key, part):
    normal_part = jnp.clip(jax.random.normal(key, (HD, D), jnp.float32), -6.0, 6.0)
    column_index = jnp.arange(D).astype(jnp.float32)
    rising = 3.0 ** (column_index / max(D - 1, 1))
    return (normal_part * rising[None, :] / math.sqrt(HD)).astype(jnp.bfloat16)


def draw_pool_cache(key, part):
    shape_all = (N_REQ * POOL, PAGE, 2, HD)
    return jnp.clip(jax.random.normal(key, shape_all, jnp.float32), -6.0, 6.0).astype(jnp.bfloat16)


def levels(stream_key, extent, pieces, least, high):
    loudness = 1.0
    for axis_at, shards_of in pieces:
        steps = jax.random.uniform(jax.random.fold_in(jax.random.fold_in(stream_key, 6), axis_at), (shards_of,), jnp.float32, least / len(pieces), high / len(pieces))
        loudness = loudness * jnp.repeat(jnp.exp(steps), extent[axis_at] // shards_of).reshape((-1,) + (1,) * (len(extent) - 1 - axis_at))
    return loudness


def split_up(amount, total, limit, slope):
    loads = [(1 << 20) // math.isqrt(grade ** slope) + 1 for grade in range(2, amount + 1)]
    rest, given = total - limit - (amount - 1), [1] * (amount - 1)
    while rest > 0:
        free = [i for i in range(amount - 1) if given[i] < limit]
        pool, left = sum([loads[i] for i in free]), rest
        for i in free:
            more = min(limit - given[i], max(1, left * loads[i] // pool), rest)
            given[i] = given[i] + more
            rest = rest - more
    return np.array([limit] + given)


def ragged_sizes(stream_key, count, total, limit, lean):
    if count == 2:
        one = jax.random.randint(stream_key, (), max(1, total - limit), min(limit, total - 1) + 1)
        return jnp.stack([one, total - one])
    tallies = jnp.asarray(split_up(count, total, limit, lean), jnp.int32)
    couples = (count - 1) // 2
    source_of, receiver = tallies[1:1 + 2 * couples:2], tallies[2:2 + 2 * couples:2]
    slack = jnp.minimum(source_of - 1, limit - receiver)
    shifted = jax.random.randint(jax.random.fold_in(stream_key, 1), (couples,), 0, 1 << 20) % (slack + 1)
    tallies = tallies.at[1:1 + 2 * couples:2].set(source_of - shifted).at[2:2 + 2 * couples:2].set(receiver + shifted)
    return tallies[jax.random.permutation(jax.random.fold_in(stream_key, 2), count)]


def scatter_about(key, extent, width, bound, cuts=(), kind=jnp.bfloat16):
    result = width * jax.random.normal(key, extent, jnp.float32)
    if cuts:
        result = result * levels(key, extent, cuts, -0.22, 0.18)
    return jnp.clip(result, -bound, bound).astype(kind)


def setup_inputs(seed: int = 0) -> dict:
    arg_keys = jax.random.split(jax.random.key(seed), 11)
    return {
        "tokens": scatter_about(arg_keys[0], (TOKENS, D), 1.0, 6.0, ((0, 256),)),
        "qkv_weight": draw_qkv_weight(jax.random.fold_in(arg_keys[10], 71), 0),
        "out_weight": draw_out_weight(jax.random.fold_in(arg_keys[10], 71), 0),
        "query_key_gain": jnp.clip(1.0 + 0.15 * jax.random.normal(arg_keys[3], (2, HD), jnp.float32), 0.25, 1.75),
        "post_gain": jnp.clip(1.0 + 0.15 * jax.random.normal(arg_keys[4], (D,), jnp.float32), 0.25, 1.75),
        "pool_cache": draw_pool_cache(jax.random.fold_in(arg_keys[10], 71), 0),
        "lengths": jax.vmap(lambda own: ragged_sizes(own, REQS, BLOCK, CAP * PAGE, 2))(jax.random.split(arg_keys[6], N_REQ)).reshape((N_REQ, REQS)).astype(jnp.int32),
        "prefix_pages": jax.vmap(lambda own: ragged_sizes(own, REQS, POOL, PMAX, 2))(jax.random.split(arg_keys[7], N_REQ)).reshape((N_REQ, REQS)).astype(jnp.int32),
        "pool_order": jax.vmap(lambda own: jax.random.permutation(own, POOL))(jax.random.split(arg_keys[8], N_REQ)).reshape((N_REQ, POOL)).astype(jnp.int32),
        "owners": jax.vmap(lambda own: jax.random.permutation(own, N_REQ))(jax.random.split(arg_keys[9], N_REQ)).reshape((N_REQ, REQS)).astype(jnp.int32),
    }


norm_eps = 1e-06
rope_base = 500000.0
masked_score = -1e+30

def token_layout(lengths_row, prefix_row, block_len):
    ends_at = jnp.cumsum(lengths_row).astype(jnp.int32)
    starts_at = (ends_at - lengths_row).astype(jnp.int32)
    token_ids = jnp.arange(block_len, dtype=jnp.int32)
    request_of = lax.optimization_barrier(jnp.sum((token_ids[:, None] >= ends_at[None, :]).astype(jnp.int32), axis=1))
    one_hot = (request_of[:, None] == jnp.arange(lengths_row.shape[0], dtype=jnp.int32)[None, :]).astype(jnp.int32)
    shift_of = lax.optimization_barrier(jnp.sum(one_hot * (prefix_row * PAGE - starts_at)[None, :], axis=1))
    return (request_of, (token_ids + shift_of).astype(jnp.int32), starts_at)

def slot_owner(prefix_row, order_row):
    page_ends = jnp.cumsum(prefix_row).astype(jnp.int32)
    page_ids = jnp.arange(order_row.shape[0], dtype=jnp.int32)
    page_request = lax.optimization_barrier(jnp.sum((page_ids[:, None] >= page_ends[None, :]).astype(jnp.int32), axis=1))
    matches = (order_row[None, :] == page_ids[:, None]).astype(jnp.int32)
    return lax.optimization_barrier(jnp.sum(matches * page_request[None, :], axis=1))

def rotate_heads(tensor, positions):
    half_dim = HEAD // 2
    frequency = rope_base ** (-(2.0 * jnp.arange(half_dim, dtype=jnp.float32)) / HEAD)
    angles = positions.astype(jnp.float32)[:, None] * frequency[None, :]
    cosine = jnp.cos(angles)[:, None, :]
    sine_part = jnp.sin(angles)[:, None, :]
    first_half = tensor[..., :half_dim]
    second_half = tensor[..., half_dim:]
    return jnp.concatenate([first_half * cosine - second_half * sine_part, second_half * cosine + first_half * sine_part], axis=-1)

def attend_head(queries, pool_keys, pool_values, new_keys, new_values, pool_mask, block_mask):
    score_scale = HEAD ** (-0.5)
    pool_scores = jnp.dot(queries, pool_keys.T, preferred_element_type=jnp.float32) * score_scale
    block_scores = jnp.dot(queries, new_keys.T, preferred_element_type=jnp.float32) * score_scale
    pool_scores = jnp.where(pool_mask, pool_scores, masked_score)
    block_scores = jnp.where(block_mask, block_scores, masked_score)
    row_max = jnp.maximum(lax.optimization_barrier(jnp.max(pool_scores, axis=1)), lax.optimization_barrier(jnp.max(block_scores, axis=1)))
    pool_exp = jnp.exp(pool_scores - row_max[:, None])
    block_exp = jnp.exp(block_scores - row_max[:, None])
    row_total = lax.optimization_barrier(jnp.sum(pool_exp, axis=1)) + lax.optimization_barrier(jnp.sum(block_exp, axis=1))
    pool_weights = (pool_exp / row_total[:, None]).astype(jnp.bfloat16)
    block_weights = (block_exp / row_total[:, None]).astype(jnp.bfloat16)
    mixed_out = jnp.dot(pool_weights, pool_values, preferred_element_type=jnp.float32)
    mixed_out = mixed_out + jnp.dot(block_weights, new_values, preferred_element_type=jnp.float32)
    return mixed_out.astype(jnp.bfloat16)

def build_send(kv_new, lengths_row, starts_at, owner_row):
    page_span = CAP * PAGE
    owner_count = owner_row.shape[0]
    owner_ids = jnp.arange(owner_count, dtype=jnp.int32)
    owner_pick = (owner_row[None, :] == owner_ids[:, None]).astype(jnp.int32)
    start_of = lax.optimization_barrier(jnp.sum(owner_pick * starts_at[None, :], axis=1))
    length_of = lax.optimization_barrier(jnp.sum(owner_pick * lengths_row[None, :], axis=1))
    offsets = jnp.arange(page_span, dtype=jnp.int32)
    source = (start_of[:, None] + offsets[None, :]).astype(jnp.int32)
    is_valid = offsets[None, :] < length_of[:, None]
    source = jnp.clip(source, 0, kv_new.shape[0] - 1).reshape(-1)
    taken_rows = jnp.take(kv_new, source, axis=0).reshape(owner_count, page_span, kv_new.shape[1], kv_new.shape[2])
    return jnp.where(is_valid[:, :, None, None], taken_rows, jnp.zeros_like(taken_rows))

def reference(tokens, qkv_weight, out_weight, query_key_gain, post_gain, pool_cache, lengths, prefix_pages, pool_order, owners):
    flat_weight = qkv_weight.reshape(D, 3 * HD)
    group_width = HD // N_TP

    def run_batch(operands):
        rows_in, lengths_row, prefix_row, order_row, owner_row, pool_page = operands
        block_len = rows_in.shape[0]
        request_of, positions, starts_at = token_layout(lengths_row, prefix_row, block_len)
        joined_all = jnp.dot(rows_in, flat_weight, preferred_element_type=jnp.float32).reshape(block_len, 3, HD)
        queries = joined_all[:, 0]
        keys_raw = joined_all[:, 1]
        values_raw = joined_all[:, 2]
        queries = queries * lax.rsqrt(lax.optimization_barrier(jnp.mean(queries * queries, axis=1, keepdims=True)) + norm_eps) * query_key_gain[0]
        keys_raw = keys_raw * lax.rsqrt(lax.optimization_barrier(jnp.mean(keys_raw * keys_raw, axis=1, keepdims=True)) + norm_eps) * query_key_gain[1]
        query_rot = rotate_heads(queries.reshape(block_len, HEADS, HEAD), positions).astype(jnp.bfloat16)
        key_rot = rotate_heads(keys_raw.reshape(block_len, HEADS, HEAD), positions).astype(jnp.bfloat16)
        value_new = values_raw.reshape(block_len, HEADS, HEAD).astype(jnp.bfloat16)
        key_owner = jnp.repeat(slot_owner(prefix_row, order_row), PAGE)
        pool_mask = request_of[:, None] == key_owner[None, :]
        token_ids = jnp.arange(block_len, dtype=jnp.int32)
        block_mask = (request_of[:, None] == request_of[None, :]) & (token_ids[None, :] <= token_ids[:, None])
        pool_keys = pool_page[:, :, 0, :].reshape(POOL * PAGE, HEADS, HEAD)
        pool_values = pool_page[:, :, 1, :].reshape(POOL * PAGE, HEADS, HEAD)
        head_outs = lax.map(lambda per_head: attend_head(per_head[0], per_head[1], per_head[2], per_head[3], per_head[4], pool_mask, block_mask), (jnp.moveaxis(query_rot, 1, 0), jnp.moveaxis(pool_keys, 1, 0), jnp.moveaxis(pool_values, 1, 0), jnp.moveaxis(key_rot, 1, 0), jnp.moveaxis(value_new, 1, 0)))
        attention = jnp.moveaxis(head_outs, 0, 1).reshape(block_len, HD)

        def add_group(summed, group_index):
            head_cols = lax.dynamic_slice_in_dim(attention, group_index * group_width, group_width, 1)
            weight_rows = lax.dynamic_slice_in_dim(out_weight, group_index * group_width, group_width, 0)
            partial_out = jnp.dot(head_cols, weight_rows, preferred_element_type=jnp.float32).astype(jnp.bfloat16)
            return (summed + partial_out.astype(jnp.float32), group_index)
        projected = lax.scan(add_group, jnp.zeros((block_len, D), jnp.float32), jnp.arange(N_TP, dtype=jnp.int32))[0]
        post_scale = lax.rsqrt(lax.optimization_barrier(jnp.mean(projected * projected, axis=1, keepdims=True)) + norm_eps)
        hidden_rows = (rows_in.astype(jnp.float32) + projected * post_scale * post_gain[None, :]).astype(jnp.bfloat16)
        kv_new = jnp.stack([key_rot.reshape(block_len, HD), value_new.reshape(block_len, HD)], axis=1)
        outgoing = build_send(kv_new, lengths_row, starts_at, owner_row)
        return (hidden_rows, outgoing)
    batches = tokens.reshape(N_REQ, BLOCK, D)
    pool_batches = pool_cache.reshape(N_REQ, POOL, PAGE, 2, HD)
    hidden_all, outgoing_all = lax.map(run_batch, (batches, lengths, prefix_pages, pool_order, owners, pool_batches))
    handed_pages = jnp.swapaxes(outgoing_all, 0, 1).reshape(N_REQ * N_REQ * CAP, PAGE, 2, HD)
    return (hidden_all.reshape(TOKENS, D), handed_pages)
```

```python
import functools

import jax
import jax.numpy as jnp
from jax import lax
from jax.experimental import pallas as pl
from jax.experimental.pallas import tpu as pltpu
from jax.sharding import PartitionSpec as P

HEADS = 32
HEAD = 128
PAGE = 128
CAP = 2
QTILE = 128
CHUNK = 512

norm_eps = 1e-06
rope_base = 500000.0
masked_score = -1e30
log2_e = 1.4426950408889634
MESH = pl.DeviceIdType.MESH


def token_layout(lengths_row, prefix_row, block_len):
    ends_at = jnp.cumsum(lengths_row)
    starts_at = ends_at - lengths_row
    token_ids = jnp.arange(block_len, dtype=jnp.int32)
    request_of = jnp.sum((token_ids[:, None] >= ends_at[None, :]).astype(jnp.int32), axis=1)
    one_hot = (
        request_of[:, None] == jnp.arange(lengths_row.shape[0], dtype=jnp.int32)[None, :]
    ).astype(jnp.int32)
    shift_of = jnp.sum(one_hot * (prefix_row * PAGE - starts_at)[None, :], axis=1)
    return (request_of, token_ids + shift_of, starts_at)


def rotate_heads(tensor, cosine, sine_part):
    half_dim = HEAD // 2
    first_half = tensor[..., :half_dim]
    second_half = tensor[..., half_dim:]
    return jnp.concatenate(
        [
            first_half * cosine - second_half * sine_part,
            second_half * cosine + first_half * sine_part,
        ],
        axis=-1,
    )


def sum_kernel(count, x_ref, o_ref, slots, send_sem, recv_sem):
    me = lax.axis_index("tp")
    barrier = pltpu.get_barrier_semaphore()
    for d in range(1, count):
        pl.semaphore_signal(
            barrier, inc=1, device_id={"tp": lax.rem(me + d, count)}, device_id_type=MESH
        )
    pl.semaphore_wait(barrier, count - 1)
    copies = []
    for d in range(1, count):
        copy = pltpu.make_async_remote_copy(
            src_ref=x_ref,
            dst_ref=slots.at[d - 1],
            send_sem=send_sem.at[d - 1],
            recv_sem=recv_sem.at[d - 1],
            device_id={"tp": lax.rem(me + d, count)},
            device_id_type=MESH,
        )
        copy.start()
        copies.append(copy)
    for copy in copies:
        copy.wait()
    total = x_ref[...]
    for d in range(1, count):
        total = total + slots[d - 1]
    o_ref[...] = total


def sum_over_tp(x, count):
    return pl.pallas_call(
        functools.partial(sum_kernel, count),
        out_shape=jax.ShapeDtypeStruct(x.shape, x.dtype),
        in_specs=[pl.BlockSpec(memory_space=pltpu.VMEM)],
        out_specs=pl.BlockSpec(memory_space=pltpu.VMEM),
        scratch_shapes=[
            pltpu.VMEM((count - 1,) + x.shape, x.dtype),
            pltpu.SemaphoreType.DMA((count - 1,)),
            pltpu.SemaphoreType.DMA((count - 1,)),
        ],
        compiler_params=pltpu.CompilerParams(collective_id=0, has_side_effects=True),
        cost_estimate=pl.CostEstimate(flops=100000, bytes_accessed=20000000, transcendentals=0),
        name="sum_squares",
    )(x)


def attend_kernel(
    bounds_ref, q_ref, kn_ref, vn_ref, kt_ref, vp_ref, row_ref, col_ref, key_ref, o_ref
):
    block_len, width = q_ref.shape
    heads_here = width // HEAD
    scale = HEAD ** (-0.5) * log2_e
    for i in range(block_len // QTILE):
        r0, r1 = i * QTILE, (i + 1) * QTILE
        k0 = max(0, r0 - CAP * PAGE)
        row_req = row_ref[r0:r1, :]
        row_ids = lax.broadcasted_iota(jnp.int32, (QTILE, r1 - k0), 0) + r0
        col_ids = lax.broadcasted_iota(jnp.int32, (QTILE, r1 - k0), 1) + k0
        block_mask = (row_req == col_ref[:, k0:r1]) & (col_ids <= row_ids)
        carry = []
        for h in range(heads_here):
            cols = slice(h * HEAD, (h + 1) * HEAD)
            scores = lax.dot_general(
                q_ref[r0:r1, cols],
                kn_ref[k0:r1, cols],
                (((1,), (1,)), ((), ())),
                preferred_element_type=jnp.float32,
            )
            scores = jnp.where(block_mask, scores * scale, masked_score)
            top = jnp.max(scores, axis=1, keepdims=True)
            weights = jnp.exp2(scores - top)
            total = jnp.sum(weights, axis=1, keepdims=True)
            mixed = jnp.dot(
                weights.astype(jnp.bfloat16), vn_ref[k0:r1, cols], preferred_element_type=jnp.float32
            )
            carry += [top, total, mixed]

        def step(j, carry):
            off = pl.multiple_of(j * CHUNK, CHUNK)
            mask = row_req == key_ref[:, pl.ds(off, CHUNK)]
            out = []
            for h in range(heads_here):
                cols = slice(h * HEAD, (h + 1) * HEAD)
                top, total, mixed = carry[3 * h : 3 * h + 3]
                scores = jnp.dot(
                    q_ref[r0:r1, cols],
                    kt_ref[cols, pl.ds(off, CHUNK)],
                    preferred_element_type=jnp.float32,
                )
                scores = jnp.where(mask, scores * scale, masked_score)
                new_top = jnp.maximum(top, jnp.max(scores, axis=1, keepdims=True))
                fade = jnp.exp2(top - new_top)
                weights = jnp.exp2(scores - new_top)
                total = total * fade + jnp.sum(weights, axis=1, keepdims=True)
                mixed = mixed * fade + jnp.dot(
                    weights.astype(jnp.bfloat16),
                    vp_ref[pl.ds(off, CHUNK), cols],
                    preferred_element_type=jnp.float32,
                )
                out += [new_top, total, mixed]
            return tuple(out)

        carry = lax.fori_loop(bounds_ref[0, i], bounds_ref[1, i], step, tuple(carry))
        for h in range(heads_here):
            cols = slice(h * HEAD, (h + 1) * HEAD)
            o_ref[r0:r1, cols] = (carry[3 * h + 2] / carry[3 * h + 1]).astype(jnp.bfloat16)


def attend(bounds, q, kn, vn, kt, vp, row_req, col_req, key_req):
    vmem = pl.BlockSpec(memory_space=pltpu.VMEM)
    return pl.pallas_call(
        attend_kernel,
        out_shape=jax.ShapeDtypeStruct(q.shape, jnp.bfloat16),
        in_specs=[pl.BlockSpec(memory_space=pltpu.SMEM)] + [vmem] * 8,
        out_specs=vmem,
        cost_estimate=pl.CostEstimate(
            flops=4000000000, bytes_accessed=40000000, transcendentals=4000000
        ),
        name="paged_attention",
    )(bounds, q, kn, vn, kt, vp, row_req, col_req, key_req)


def moves(n_y, n_x, dy, dx, dc):
    pairs = []
    for y in range(n_y):
        for x in range(n_x):
            for c in range(2):
                src = (y * n_x + x) * 2 + c
                dst = ((y ^ dy) * n_x + (x + dx) % n_x) * 2 + (c ^ dc)
                pairs.append((src, dst))
    return pairs


def body(
    tokens,
    qkv_weight,
    out_weight,
    query_key_gain,
    post_gain,
    pool_cache,
    lengths,
    prefix_pages,
    pool_order,
    owners,
):
    n_req = lax.axis_size("req")
    n_tp = lax.axis_size("tp")
    n_y, n_x = 2, n_req // 4
    me = lax.axis_index("req")
    my_y, my_x, my_c = me // (2 * n_x), (me // 2) % n_x, me % 2

    def shift(value, dy, dx, dc):
        return lax.ppermute(value, "req", moves(n_y, n_x, dy, dx, dc))

    def slot_of(dy, dx, dc):
        return ((my_y ^ dy) * n_x + (my_x - dx + n_x) % n_x) * 2 + (my_c ^ dc)

    local_rows = qkv_weight.shape[0]
    local_width = qkv_weight.shape[2]
    qkv_width = 3 * local_width
    heads_here = local_width // HEAD
    block_tokens = lax.all_gather(tokens, "tp", axis=0, tiled=True)
    block_len = block_tokens.shape[0]

    own = jnp.concatenate([qkv_weight.reshape(local_rows, qkv_width), out_weight.T], axis=1)
    pieces = []
    other = shift(own, 1, 0, 0)
    pair = jnp.stack([own, other])
    from_left = shift(pair, 0, 1, 0)
    from_right = shift(pair, 0, -1, 0)
    far_a = shift(from_left[0], 0, 1, 0)
    far_b = shift(from_right[1], 0, -1, 0)
    far = jnp.stack([far_a, far_b])
    for dx, both in ((0, pair), (1, from_left), (-1, from_right), (2, far)):
        swapped = shift(both, 0, 0, 1)
        for dc, held in ((0, both), (1, swapped)):
            for dy in range(2):
                pieces.append((slot_of(dy, dx, dc), held[dy]))
    qkv_full = jnp.zeros((n_req * local_rows, qkv_width), jnp.bfloat16)
    out_full = jnp.zeros((n_req * local_rows, local_width), jnp.bfloat16)
    for slot, piece in pieces:
        qkv_full = lax.dynamic_update_slice(qkv_full, piece[:, :qkv_width], (slot * local_rows, 0))
        out_full = lax.dynamic_update_slice(out_full, piece[:, qkv_width:], (slot * local_rows, 0))

    lengths_row = lengths[0]
    prefix_row = prefix_pages[0]
    order_row = pool_order[0]
    request_of, positions, starts_at = token_layout(lengths_row, prefix_row, block_len)
    half_dim = HEAD // 2
    frequency = rope_base ** (-(2.0 * jnp.arange(half_dim, dtype=jnp.float32)) / HEAD)
    angles = positions.astype(jnp.float32)[:, None] * frequency[None, :]
    cosine = jnp.cos(angles)[:, None, :]
    sine_part = jnp.sin(angles)[:, None, :]

    pool_count = pool_cache.shape[0]
    page_ends = jnp.cumsum(prefix_row)
    page_starts = page_ends - prefix_row
    page_ids = jnp.arange(pool_count, dtype=jnp.int32)
    page_request = jnp.sum((page_ids[:, None] >= page_ends[None, :]).astype(jnp.int32), axis=1)
    key_req = jnp.repeat(page_request, PAGE)[None, :]
    pool_keys = jnp.take(pool_cache[:, :, 0, :], order_row, axis=0)
    pool_values = jnp.take(pool_cache[:, :, 1, :], order_row, axis=0)
    keys_t = pool_keys.reshape(pool_count * PAGE, local_width).T
    pool_values = pool_values.reshape(pool_count * PAGE, local_width)
    tiles = block_len // QTILE
    first_req = request_of.reshape(tiles, QTILE)[:, 0]
    last_req = request_of.reshape(tiles, QTILE)[:, -1]
    req_ids = jnp.arange(lengths_row.shape[0], dtype=jnp.int32)
    low = jnp.sum(jnp.where(first_req[:, None] == req_ids[None, :], page_starts[None, :], 0), axis=1)
    high = jnp.sum(jnp.where(last_req[:, None] == req_ids[None, :], page_ends[None, :], 0), axis=1)
    per_chunk = CHUNK // PAGE
    bounds = jnp.stack([low // per_chunk, (high + per_chunk - 1) // per_chunk]).astype(jnp.int32)

    joined_all = jnp.dot(block_tokens, qkv_full, preferred_element_type=jnp.float32)
    queries = joined_all[:, :local_width]
    keys_raw = joined_all[:, local_width : 2 * local_width]
    values_raw = joined_all[:, 2 * local_width :]
    local_sums = jnp.stack(
        [jnp.sum(queries * queries, axis=1), jnp.sum(keys_raw * keys_raw, axis=1)]
    )
    global_sums = sum_over_tp(local_sums, n_tp)
    inverse = lax.rsqrt(global_sums / (HEADS * HEAD) + norm_eps)
    queries = queries * inverse[0][:, None] * query_key_gain[0]
    keys_raw = keys_raw * inverse[1][:, None] * query_key_gain[1]
    query_rot = (
        rotate_heads(queries.reshape(block_len, heads_here, HEAD), cosine, sine_part)
        .astype(jnp.bfloat16)
        .reshape(block_len, local_width)
    )
    key_rot = (
        rotate_heads(keys_raw.reshape(block_len, heads_here, HEAD), cosine, sine_part)
        .astype(jnp.bfloat16)
        .reshape(block_len, local_width)
    )
    value_new = values_raw.astype(jnp.bfloat16)

    page_span = CAP * PAGE
    owner_pick = (owners[0][None, :] == jnp.arange(n_req, dtype=jnp.int32)[:, None]).astype(jnp.int32)
    start_of = jnp.sum(owner_pick * starts_at[None, :], axis=1)
    length_of = jnp.sum(owner_pick * lengths_row[None, :], axis=1)
    offsets = jnp.arange(page_span, dtype=jnp.int32)
    source = jnp.where(
        offsets[None, :] < length_of[:, None], start_of[:, None] + offsets[None, :], -1
    ).reshape(-1)
    token_ids = jnp.arange(block_len, dtype=jnp.int32)
    select = (source[:, None] == token_ids[None, :]).astype(jnp.bfloat16)
    kv_new = jnp.concatenate([key_rot, value_new], axis=1)
    outgoing = jnp.dot(select, kv_new, preferred_element_type=jnp.float32).astype(jnp.bfloat16)
    arrived = jnp.zeros((n_req * page_span, 2 * local_width), jnp.bfloat16)
    for dy in range(2):
        for dx in range(n_x):
            for dc in range(2):
                to = slot_of(dy, -dx, dc)
                piece = lax.dynamic_slice(
                    outgoing, (to * page_span, 0), (page_span, 2 * local_width)
                )
                if dy or dx or dc:
                    piece = shift(piece, dy, dx, dc)
                arrived = lax.dynamic_update_slice(
                    arrived, piece, (slot_of(dy, dx, dc) * page_span, 0)
                )
    handed_pages = arrived.reshape(n_req * CAP, PAGE, 2, local_width)

    attention = attend(
        bounds,
        query_rot,
        key_rot,
        value_new,
        keys_t,
        pool_values,
        request_of[:, None],
        request_of[None, :],
        key_req,
    )
    partial = lax.dot_general(
        attention, out_full, (((1,), (1,)), ((), ())), preferred_element_type=jnp.float32
    ).astype(jnp.bfloat16)
    projected = lax.psum_scatter(partial, "tp", scatter_dimension=0, tiled=True).astype(jnp.float32)
    post_scale = lax.rsqrt(jnp.mean(projected * projected, axis=1, keepdims=True) + norm_eps)
    hidden = (tokens.astype(jnp.float32) + projected * post_scale * post_gain[None, :]).astype(
        jnp.bfloat16
    )
    return (hidden, handed_pages)


def solution(mesh):
    in_specs = (
        P(("req", "tp"), None),
        P("req", None, "tp"),
        P("tp", "req"),
        P(None, "tp"),
        P(),
        P("req", None, None, "tp"),
        P("req", None),
        P("req", None),
        P("req", None),
        P("req", None),
    )
    out_specs = (P(("req", "tp"), None), P("req", None, None, "tp"))
    return jax.shard_map(body, mesh=mesh, in_specs=in_specs, out_specs=out_specs, check_vma=False)
```

```python
import functools

import jax
import jax.numpy as jnp
from jax import lax
from jax.experimental import pallas as pl
from jax.experimental.pallas import tpu as pltpu
from jax.sharding import PartitionSpec as P

HEADS = 32
HEAD = 128
PAGE = 128
CAP = 2
QTILE = 128
CHUNK = 512

norm_eps = 1e-06
rope_base = 500000.0
masked_score = -1e30
log2_e = 1.4426950408889634
MESH = pl.DeviceIdType.MESH


def token_layout(lengths_row, prefix_row, block_len):
    ends_at = jnp.cumsum(lengths_row)
    starts_at = ends_at - lengths_row
    token_ids = jnp.arange(block_len, dtype=jnp.int32)
    request_of = jnp.sum((token_ids[:, None] >= ends_at[None, :]).astype(jnp.int32), axis=1)
    one_hot = (
        request_of[:, None] == jnp.arange(lengths_row.shape[0], dtype=jnp.int32)[None, :]
    ).astype(jnp.int32)
    shift_of = jnp.sum(one_hot * (prefix_row * PAGE - starts_at)[None, :], axis=1)
    return (request_of, token_ids + shift_of, starts_at)


def rotate_heads(tensor, cosine, sine_part):
    half_dim = HEAD // 2
    first_half = tensor[..., :half_dim]
    second_half = tensor[..., half_dim:]
    return jnp.concatenate(
        [
            first_half * cosine - second_half * sine_part,
            second_half * cosine + first_half * sine_part,
        ],
        axis=-1,
    )


def sum_kernel(count, x_ref, o_ref, slots, send_sem, recv_sem):
    me = lax.axis_index("tp")
    barrier = pltpu.get_barrier_semaphore()
    for d in range(1, count):
        pl.semaphore_signal(
            barrier, inc=1, device_id={"tp": lax.rem(me + d, count)}, device_id_type=MESH
        )
    pl.semaphore_wait(barrier, count - 1)
    copies = []
    for d in range(1, count):
        copy = pltpu.make_async_remote_copy(
            src_ref=x_ref,
            dst_ref=slots.at[d - 1],
            send_sem=send_sem.at[d - 1],
            recv_sem=recv_sem.at[d - 1],
            device_id={"tp": lax.rem(me + d, count)},
            device_id_type=MESH,
        )
        copy.start()
        copies.append(copy)
    for copy in copies:
        copy.wait()
    total = x_ref[...]
    for d in range(1, count):
        total = total + slots[d - 1]
    o_ref[...] = total


def sum_over_tp(x, count):
    return pl.pallas_call(
        functools.partial(sum_kernel, count),
        out_shape=jax.ShapeDtypeStruct(x.shape, x.dtype),
        in_specs=[pl.BlockSpec(memory_space=pltpu.VMEM)],
        out_specs=pl.BlockSpec(memory_space=pltpu.VMEM),
        scratch_shapes=[
            pltpu.VMEM((count - 1,) + x.shape, x.dtype),
            pltpu.SemaphoreType.DMA((count - 1,)),
            pltpu.SemaphoreType.DMA((count - 1,)),
        ],
        compiler_params=pltpu.CompilerParams(collective_id=0, has_side_effects=True),
        cost_estimate=pl.CostEstimate(flops=100000, bytes_accessed=20000000, transcendentals=0),
        name="sum_squares",
    )(x)


def attend_kernel(
    bounds_ref, q_ref, kn_ref, vn_ref, kt_ref, vp_ref, row_ref, col_ref, key_ref, o_ref
):
    block_len, width = q_ref.shape
    heads_here = width // HEAD
    scale = HEAD ** (-0.5) * log2_e
    window = CAP * PAGE + QTILE

    def tile(i, _):
        r0 = pl.multiple_of(i * QTILE, QTILE)
        k0 = pl.multiple_of(jnp.maximum(i - CAP, 0) * QTILE, QTILE)
        tile_rows, tile_keys = pl.ds(r0, QTILE), pl.ds(k0, window)
        row_req = row_ref[tile_rows, :]
        row_ids = lax.broadcasted_iota(jnp.int32, (QTILE, window), 0) + r0
        col_ids = lax.broadcasted_iota(jnp.int32, (QTILE, window), 1) + k0
        block_mask = (row_req == col_ref[:, tile_keys]) & (col_ids <= row_ids)
        carry = []
        for h in range(heads_here):
            cols = slice(h * HEAD, (h + 1) * HEAD)
            scores = lax.dot_general(
                q_ref[tile_rows, cols],
                kn_ref[tile_keys, cols],
                (((1,), (1,)), ((), ())),
                preferred_element_type=jnp.float32,
            )
            scores = jnp.where(block_mask, scores * scale, masked_score)
            top = jnp.max(scores, axis=1, keepdims=True)
            weights = jnp.exp2(scores - top)
            total = jnp.sum(weights, axis=1, keepdims=True)
            mixed = jnp.dot(
                weights.astype(jnp.bfloat16), vn_ref[tile_keys, cols], preferred_element_type=jnp.float32
            )
            carry += [top, total, mixed]

        def step(j, carry):
            off = pl.multiple_of(j * CHUNK, CHUNK)
            mask = row_req == key_ref[:, pl.ds(off, CHUNK)]
            out = []
            for h in range(heads_here):
                cols = slice(h * HEAD, (h + 1) * HEAD)
                top, total, mixed = carry[3 * h : 3 * h + 3]
                scores = jnp.dot(
                    q_ref[tile_rows, cols],
                    kt_ref[cols, pl.ds(off, CHUNK)],
                    preferred_element_type=jnp.float32,
                )
                scores = jnp.where(mask, scores * scale, masked_score)
                new_top = jnp.maximum(top, jnp.max(scores, axis=1, keepdims=True))
                fade = jnp.exp2(top - new_top)
                weights = jnp.exp2(scores - new_top)
                total = total * fade + jnp.sum(weights, axis=1, keepdims=True)
                mixed = mixed * fade + jnp.dot(
                    weights.astype(jnp.bfloat16),
                    vp_ref[pl.ds(off, CHUNK), cols],
                    preferred_element_type=jnp.float32,
                )
                out += [new_top, total, mixed]
            return tuple(out)

        carry = lax.fori_loop(bounds_ref[0, i], bounds_ref[1, i], step, tuple(carry))
        for h in range(heads_here):
            cols = slice(h * HEAD, (h + 1) * HEAD)
            o_ref[tile_rows, cols] = (carry[3 * h + 2] / carry[3 * h + 1]).astype(jnp.bfloat16)
        return 0

    lax.fori_loop(0, block_len // QTILE, tile, 0)


def attend(bounds, q, kn, vn, kt, vp, row_req, col_req, key_req):
    vmem = pl.BlockSpec(memory_space=pltpu.VMEM)
    return pl.pallas_call(
        attend_kernel,
        out_shape=jax.ShapeDtypeStruct(q.shape, jnp.bfloat16),
        in_specs=[pl.BlockSpec(memory_space=pltpu.SMEM)] + [vmem] * 8,
        out_specs=vmem,
        cost_estimate=pl.CostEstimate(
            flops=4000000000, bytes_accessed=40000000, transcendentals=4000000
        ),
        name="paged_attention",
    )(bounds, q, kn, vn, kt, vp, row_req, col_req, key_req)


def gather_kernel(
    n_z, n_x, tok_ref, wq_ref, wo_ref, toks, wqs, wos, send_sem, recv_sem, local_sem
):
    tp, req = lax.axis_index("tp"), lax.axis_index("req")
    y, z = tp // n_z, lax.rem(tp, n_z)
    high, x, core = req // (2 * n_x), lax.rem(req // 2, n_x), lax.rem(req, 2)

    def token_slot(yy, dz):
        return yy * n_z + lax.rem(z + dz + n_z, n_z)

    def weight_slot(hh, dx, cc):
        return (hh * n_x + lax.rem(x + dx + n_x, n_x)) * 2 + cc

    up, down, across = (
        {"tp": token_slot(y, 1), "req": req},
        {"tp": token_slot(y, -1), "req": req},
        {"tp": token_slot(1 - y, 0), "req": req},
    )
    far, right, left, twin = (
        {"tp": tp, "req": weight_slot(1 - high, 0, core)},
        {"tp": tp, "req": weight_slot(high, 1, core)},
        {"tp": tp, "req": weight_slot(high, -1, core)},
        {"tp": tp, "req": weight_slot(high, 0, 1 - core)},
    )
    peers = (up, down, across, far, right, left, twin)

    barrier = pltpu.get_barrier_semaphore()
    for peer in peers:
        pl.semaphore_signal(barrier, inc=1, device_id=peer, device_id_type=MESH)
    pl.semaphore_wait(barrier, len(peers))

    copies = {}

    def push(name, src, dst, peer):
        index = len(copies)
        copies[name] = pltpu.make_async_remote_copy(
            src_ref=src,
            dst_ref=dst,
            send_sem=send_sem.at[index],
            recv_sem=recv_sem.at[index],
            device_id=peer,
            device_id_type=MESH,
        )
        copies[name].start()

    arrived = set()

    def await_one(name):
        copies[name].wait_recv()
        arrived.add(name)

    half = tok_ref.shape[1] // 2

    def send_token(name, part, slot, peer, own=False):
        cols = pl.ds(part * half, half)
        dst = toks.at[slot, :, cols]
        push((name, part), tok_ref.at[:, cols] if own else dst, dst, peer)

    rows = wq_ref.shape[0]

    def send_weight(name, slot, peer, own=False, part=None):
        span = pl.ds(0, rows) if part is None else pl.ds(part * (rows // 2), rows // 2)
        for tag, ref, out in (("q", wq_ref, wqs), ("o", wo_ref, wos)):
            dst = out.at[slot, span, :]
            push((name, tag), ref if own else dst, dst, peer)

    def await_weight(name):
        await_one((name, "q"))
        await_one((name, "o"))

    own_slot = token_slot(y, 0)
    own_weight = weight_slot(high, 0, core)
    for part in range(2):
        send_token("up0", part, own_slot, up, own=True)
        send_token("down0", part, own_slot, down, own=True)
        send_token("across0", part, own_slot, across, own=True)
    send_weight("right0", own_weight, right, own=True)
    send_weight("left0", own_weight, left, own=True)
    send_weight("far0", own_weight, far, own=True)
    send_weight("twin0", own_weight, twin, own=True)
    locals_ = [
        pltpu.make_async_copy(tok_ref, toks.at[own_slot], local_sem.at[0]),
        pltpu.make_async_copy(wq_ref, wqs.at[own_weight], local_sem.at[1]),
        pltpu.make_async_copy(wo_ref, wos.at[own_weight], local_sem.at[2]),
    ]
    for copy in locals_:
        copy.start()

    for part in range(2):
        await_one(("up0", part))
        send_token("up1", part, token_slot(y, -1), up)
        await_one(("down0", part))
        send_token("down1", part, token_slot(y, 1), down)
        await_one(("across0", part))
        send_token("pair_up0", part, token_slot(1 - y, 0), up)
        send_token("pair_down0", part, token_slot(1 - y, 0), down)

    await_weight("right0")
    send_weight("right1", weight_slot(high, -1, core), right, part=0)
    send_weight("twin1", weight_slot(high, -1, core), twin)
    await_weight("left0")
    send_weight("left1", weight_slot(high, 1, core), left, part=1)
    send_weight("twin2", weight_slot(high, 1, core), twin)
    await_weight("far0")
    send_weight("far_right0", weight_slot(1 - high, 0, core), right)
    send_weight("far_left0", weight_slot(1 - high, 0, core), left)
    send_weight("twin3", weight_slot(1 - high, 0, core), twin)

    for part in range(2):
        await_one(("up1", part))
        send_token("up2", part, token_slot(y, -2), up)
        send_token("across1", part, token_slot(y, -2), across)
        await_one(("down1", part))
        send_token("down2", part, token_slot(y, 2), down)
        await_one(("pair_down0", part))
        send_token("pair_down1", part, token_slot(1 - y, 1), down)

    await_weight("right1")
    await_weight("left1")
    send_weight("twin4", weight_slot(high, 2, core), twin)
    await_weight("far_right0")
    send_weight("far_right1", weight_slot(1 - high, -1, core), right, part=0)
    send_weight("twin5", weight_slot(1 - high, -1, core), twin)
    await_weight("far_left0")
    send_weight("far_left1", weight_slot(1 - high, 1, core), left, part=1)
    send_weight("twin6", weight_slot(1 - high, 1, core), twin)

    for part in range(2):
        await_one(("up2", part))
        send_token("up3", part, token_slot(y, -3), up)
        send_token("across2", part, token_slot(y, -3), across)
        await_one(("down2", part))
        send_token("across3", part, token_slot(y, 3), across)

    await_weight("far_right1")
    await_weight("far_left1")
    send_weight("twin7", weight_slot(1 - high, 2, core), twin)

    for part in range(2):
        await_one(("up3", part))
        send_token("across4", part, token_slot(y, -4), across)

    for name in copies:
        if name not in arrived:
            copies[name].wait_recv()
    for name in copies:
        copies[name].wait_send()
    for copy in locals_:
        copy.wait()


def gather_all(tokens, qkv_rows, out_rows, n_tp, n_req):
    vmem = pl.BlockSpec(memory_space=pltpu.VMEM)
    hbm = pl.BlockSpec(memory_space=pl.ANY)
    copies = 30 + 34
    return pl.pallas_call(
        functools.partial(gather_kernel, n_tp // 2, n_req // 4),
        out_shape=[
            jax.ShapeDtypeStruct((n_tp,) + tokens.shape, tokens.dtype),
            jax.ShapeDtypeStruct((n_req,) + qkv_rows.shape, qkv_rows.dtype),
            jax.ShapeDtypeStruct((n_req,) + out_rows.shape, out_rows.dtype),
        ],
        in_specs=[vmem] * 3,
        out_specs=[hbm] * 3,
        scratch_shapes=[
            pltpu.SemaphoreType.DMA((copies,)),
            pltpu.SemaphoreType.DMA((copies,)),
            pltpu.SemaphoreType.DMA((3,)),
        ],
        compiler_params=pltpu.CompilerParams(collective_id=1, has_side_effects=True),
        name="gather_all",
    )(tokens, qkv_rows, out_rows)


def body(
    tokens,
    qkv_weight,
    out_weight,
    query_key_gain,
    post_gain,
    pool_cache,
    lengths,
    prefix_pages,
    pool_order,
    owners,
):
    n_req = lax.axis_size("req")
    n_tp = lax.axis_size("tp")
    local_rows = qkv_weight.shape[0]
    local_width = qkv_weight.shape[2]
    qkv_width = 3 * local_width
    heads_here = local_width // HEAD
    block_tokens, qkv_full, out_full = gather_all(
        tokens, qkv_weight.reshape(local_rows, qkv_width), out_weight.T, n_tp, n_req
    )
    block_tokens = block_tokens.reshape(n_tp * tokens.shape[0], tokens.shape[1])
    qkv_full = qkv_full.reshape(n_req * local_rows, qkv_width)
    out_full = out_full.reshape(n_req * local_rows, local_width)
    block_len = block_tokens.shape[0]

    lengths_row = lengths[0]
    prefix_row = prefix_pages[0]
    order_row = pool_order[0]
    request_of, positions, starts_at = token_layout(lengths_row, prefix_row, block_len)
    half_dim = HEAD // 2
    frequency = rope_base ** (-(2.0 * jnp.arange(half_dim, dtype=jnp.float32)) / HEAD)
    angles = positions.astype(jnp.float32)[:, None] * frequency[None, :]
    cosine = jnp.cos(angles)[:, None, :]
    sine_part = jnp.sin(angles)[:, None, :]

    pool_count = pool_cache.shape[0]
    page_ends = jnp.cumsum(prefix_row)
    page_starts = page_ends - prefix_row
    page_ids = jnp.arange(pool_count, dtype=jnp.int32)
    page_request = jnp.sum((page_ids[:, None] >= page_ends[None, :]).astype(jnp.int32), axis=1)
    key_req = jnp.repeat(page_request, PAGE)[None, :]
    pool_keys = jnp.take(pool_cache[:, :, 0, :], order_row, axis=0)
    pool_values = jnp.take(pool_cache[:, :, 1, :], order_row, axis=0)
    keys_t = pool_keys.reshape(pool_count * PAGE, local_width).T
    pool_values = pool_values.reshape(pool_count * PAGE, local_width)
    tiles = block_len // QTILE
    first_req = request_of.reshape(tiles, QTILE)[:, 0]
    last_req = request_of.reshape(tiles, QTILE)[:, -1]
    req_ids = jnp.arange(lengths_row.shape[0], dtype=jnp.int32)
    low = jnp.sum(jnp.where(first_req[:, None] == req_ids[None, :], page_starts[None, :], 0), axis=1)
    high = jnp.sum(jnp.where(last_req[:, None] == req_ids[None, :], page_ends[None, :], 0), axis=1)
    per_chunk = CHUNK // PAGE
    bounds = jnp.stack([low // per_chunk, (high + per_chunk - 1) // per_chunk]).astype(jnp.int32)

    joined_all = jnp.dot(block_tokens, qkv_full, preferred_element_type=jnp.float32)
    queries = joined_all[:, :local_width]
    keys_raw = joined_all[:, local_width : 2 * local_width]
    values_raw = joined_all[:, 2 * local_width :]
    local_sums = jnp.stack(
        [jnp.sum(queries * queries, axis=1), jnp.sum(keys_raw * keys_raw, axis=1)]
    )
    global_sums = sum_over_tp(local_sums, n_tp)
    inverse = lax.rsqrt(global_sums / (HEADS * HEAD) + norm_eps)
    queries = queries * inverse[0][:, None] * query_key_gain[0]
    keys_raw = keys_raw * inverse[1][:, None] * query_key_gain[1]
    query_rot = (
        rotate_heads(queries.reshape(block_len, heads_here, HEAD), cosine, sine_part)
        .astype(jnp.bfloat16)
        .reshape(block_len, local_width)
    )
    key_rot = (
        rotate_heads(keys_raw.reshape(block_len, heads_here, HEAD), cosine, sine_part)
        .astype(jnp.bfloat16)
        .reshape(block_len, local_width)
    )
    value_new = values_raw.astype(jnp.bfloat16)

    page_span = CAP * PAGE
    owner_pick = (owners[0][None, :] == jnp.arange(n_req, dtype=jnp.int32)[:, None]).astype(jnp.int32)
    start_of = jnp.sum(owner_pick * starts_at[None, :], axis=1)
    length_of = jnp.sum(owner_pick * lengths_row[None, :], axis=1)
    offsets = jnp.arange(page_span, dtype=jnp.int32)
    source = jnp.where(
        offsets[None, :] < length_of[:, None], start_of[:, None] + offsets[None, :], -1
    ).reshape(-1)
    token_ids = jnp.arange(block_len, dtype=jnp.int32)
    select = (source[:, None] == token_ids[None, :]).astype(jnp.bfloat16)
    kv_new = jnp.concatenate([key_rot, value_new], axis=1)
    outgoing = jnp.dot(select, kv_new, preferred_element_type=jnp.float32).astype(jnp.bfloat16)
    arrived = lax.all_to_all(
        outgoing.reshape(n_req, page_span, 2 * local_width),
        "req",
        split_axis=0,
        concat_axis=0,
        tiled=True,
    )
    handed_pages = arrived.reshape(n_req * CAP, PAGE, 2, local_width)

    attention = attend(
        bounds,
        query_rot,
        key_rot,
        value_new,
        keys_t,
        pool_values,
        request_of[:, None],
        request_of[None, :],
        key_req,
    )
    partial = lax.dot_general(
        attention, out_full, (((1,), (1,)), ((), ())), preferred_element_type=jnp.float32
    ).astype(jnp.bfloat16)
    projected = lax.psum_scatter(partial, "tp", scatter_dimension=0, tiled=True).astype(jnp.float32)
    post_scale = lax.rsqrt(jnp.mean(projected * projected, axis=1, keepdims=True) + norm_eps)
    hidden = (tokens.astype(jnp.float32) + projected * post_scale * post_gain[None, :]).astype(
        jnp.bfloat16
    )
    return (hidden, handed_pages)


def solution(mesh):
    in_specs = (
        P(("req", "tp"), None),
        P("req", None, "tp"),
        P("tp", "req"),
        P(None, "tp"),
        P(),
        P("req", None, None, "tp"),
        P("req", None),
        P("req", None),
        P("req", None),
        P("req", None),
    )
    out_specs = (P(("req", "tp"), None), P("req", None, None, "tp"))
    return jax.shard_map(body, mesh=mesh, in_specs=in_specs, out_specs=out_specs, check_vma=False)
```

```python
import functools

import jax
import jax.numpy as jnp
from jax import lax
from jax.experimental import pallas as pl
from jax.experimental.pallas import tpu as pltpu
from jax.sharding import PartitionSpec as P

HEADS = 32
HEAD = 128
PAGE = 128
CAP = 2
QTILE = 128
CHUNK = 512

norm_eps = 1e-06
rope_base = 500000.0
masked_score = -1e30
log2_e = 1.4426950408889634
MESH = pl.DeviceIdType.MESH


def token_layout(lengths_row, prefix_row, block_len):
    ends_at = jnp.cumsum(lengths_row)
    starts_at = ends_at - lengths_row
    token_ids = jnp.arange(block_len, dtype=jnp.int32)
    request_of = jnp.sum((token_ids[:, None] >= ends_at[None, :]).astype(jnp.int32), axis=1)
    one_hot = (
        request_of[:, None] == jnp.arange(lengths_row.shape[0], dtype=jnp.int32)[None, :]
    ).astype(jnp.int32)
    shift_of = jnp.sum(one_hot * (prefix_row * PAGE - starts_at)[None, :], axis=1)
    return (request_of, token_ids + shift_of, starts_at)


def rotate_heads(tensor, cosine, sine_part):
    half_dim = HEAD // 2
    first_half = tensor[..., :half_dim]
    second_half = tensor[..., half_dim:]
    return jnp.concatenate(
        [
            first_half * cosine - second_half * sine_part,
            second_half * cosine + first_half * sine_part,
        ],
        axis=-1,
    )


def sum_kernel(count, x_ref, o_ref, slots, send_sem, recv_sem):
    me = lax.axis_index("tp")
    barrier = pltpu.get_barrier_semaphore()
    for d in range(1, count):
        pl.semaphore_signal(
            barrier, inc=1, device_id={"tp": lax.rem(me + d, count)}, device_id_type=MESH
        )
    pl.semaphore_wait(barrier, count - 1)
    copies = []
    for d in range(1, count):
        copy = pltpu.make_async_remote_copy(
            src_ref=x_ref,
            dst_ref=slots.at[d - 1],
            send_sem=send_sem.at[d - 1],
            recv_sem=recv_sem.at[d - 1],
            device_id={"tp": lax.rem(me + d, count)},
            device_id_type=MESH,
        )
        copy.start()
        copies.append(copy)
    for copy in copies:
        copy.wait()
    total = x_ref[...]
    for d in range(1, count):
        total = total + slots[d - 1]
    o_ref[...] = total


def sum_over_tp(x, count):
    return pl.pallas_call(
        functools.partial(sum_kernel, count),
        out_shape=jax.ShapeDtypeStruct(x.shape, x.dtype),
        in_specs=[pl.BlockSpec(memory_space=pltpu.VMEM)],
        out_specs=pl.BlockSpec(memory_space=pltpu.VMEM),
        scratch_shapes=[
            pltpu.VMEM((count - 1,) + x.shape, x.dtype),
            pltpu.SemaphoreType.DMA((count - 1,)),
            pltpu.SemaphoreType.DMA((count - 1,)),
        ],
        compiler_params=pltpu.CompilerParams(collective_id=0, has_side_effects=True),
        cost_estimate=pl.CostEstimate(flops=100000, bytes_accessed=20000000, transcendentals=0),
        name="sum_squares",
    )(x)


def attend_kernel(
    bounds_ref, order_ref, q_ref, kn_ref, vn_ref, kp_ref, vp_ref, row_ref, col_ref, key_ref, o_ref
):
    block_len, width = q_ref.shape
    heads_here = width // HEAD
    scale = HEAD ** (-0.5) * log2_e
    window = CAP * PAGE + QTILE

    def tile(i, _):
        r0 = pl.multiple_of(i * QTILE, QTILE)
        k0 = pl.multiple_of(jnp.maximum(i - CAP, 0) * QTILE, QTILE)
        tile_rows, tile_keys = pl.ds(r0, QTILE), pl.ds(k0, window)
        row_req = row_ref[tile_rows, :]
        row_ids = lax.broadcasted_iota(jnp.int32, (QTILE, window), 0) + r0
        col_ids = lax.broadcasted_iota(jnp.int32, (QTILE, window), 1) + k0
        block_mask = (row_req == col_ref[:, tile_keys]) & (col_ids <= row_ids)
        carry = []
        for h in range(heads_here):
            cols = slice(h * HEAD, (h + 1) * HEAD)
            scores = lax.dot_general(
                q_ref[tile_rows, cols],
                kn_ref[tile_keys, cols],
                (((1,), (1,)), ((), ())),
                preferred_element_type=jnp.float32,
            )
            scores = jnp.where(block_mask, scores * scale, masked_score)
            top = jnp.max(scores, axis=1, keepdims=True)
            weights = jnp.exp2(scores - top)
            total = jnp.sum(weights, axis=1, keepdims=True)
            mixed = jnp.dot(
                weights.astype(jnp.bfloat16), vn_ref[tile_keys, cols], preferred_element_type=jnp.float32
            )
            carry += [top, total, mixed]

        def step(j, carry):
            off = pl.multiple_of(j * CHUNK, CHUNK)
            mask = row_req == key_ref[:, pl.ds(off, CHUNK)]
            pages = [
                pl.ds(pl.multiple_of(order_ref[0, j * (CHUNK // PAGE) + e] * PAGE, PAGE), PAGE)
                for e in range(CHUNK // PAGE)
            ]
            out = []
            for h in range(heads_here):
                cols = slice(h * HEAD, (h + 1) * HEAD)
                top, total, mixed = carry[3 * h : 3 * h + 3]
                scores = lax.dot_general(
                    q_ref[tile_rows, cols],
                    jnp.concatenate([kp_ref[page, cols] for page in pages], axis=0),
                    (((1,), (1,)), ((), ())),
                    preferred_element_type=jnp.float32,
                )
                scores = jnp.where(mask, scores * scale, masked_score)
                new_top = jnp.maximum(top, jnp.max(scores, axis=1, keepdims=True))
                fade = jnp.exp2(top - new_top)
                weights = jnp.exp2(scores - new_top)
                total = total * fade + jnp.sum(weights, axis=1, keepdims=True)
                mixed = mixed * fade + jnp.dot(
                    weights.astype(jnp.bfloat16),
                    jnp.concatenate([vp_ref[page, cols] for page in pages], axis=0),
                    preferred_element_type=jnp.float32,
                )
                out += [new_top, total, mixed]
            return tuple(out)

        carry = lax.fori_loop(bounds_ref[0, i], bounds_ref[1, i], step, tuple(carry))
        for h in range(heads_here):
            cols = slice(h * HEAD, (h + 1) * HEAD)
            o_ref[tile_rows, cols] = (carry[3 * h + 2] / carry[3 * h + 1]).astype(jnp.bfloat16)
        return 0

    lax.fori_loop(0, block_len // QTILE, tile, 0)


def attend(bounds, order, q, kn, vn, kp, vp, row_req, col_req, key_req):
    vmem = pl.BlockSpec(memory_space=pltpu.VMEM)
    return pl.pallas_call(
        attend_kernel,
        out_shape=jax.ShapeDtypeStruct(q.shape, jnp.bfloat16),
        in_specs=[pl.BlockSpec(memory_space=pltpu.SMEM)] * 2 + [vmem] * 8,
        out_specs=vmem,
        cost_estimate=pl.CostEstimate(
            flops=4000000000, bytes_accessed=40000000, transcendentals=4000000
        ),
        name="paged_attention",
    )(bounds, order, q, kn, vn, kp, vp, row_req, col_req, key_req)


def gather_kernel(
    n_z, n_x, tok_ref, wq_ref, wo_ref, toks, wqs, wos, send_sem, recv_sem, local_sem
):
    tp, req = lax.axis_index("tp"), lax.axis_index("req")
    y, z = tp // n_z, lax.rem(tp, n_z)
    high, x, core = req // (2 * n_x), lax.rem(req // 2, n_x), lax.rem(req, 2)

    def token_slot(yy, dz):
        return yy * n_z + lax.rem(z + dz + n_z, n_z)

    def weight_slot(hh, dx, cc):
        return (hh * n_x + lax.rem(x + dx + n_x, n_x)) * 2 + cc

    up, down, across = (
        {"tp": token_slot(y, 1), "req": req},
        {"tp": token_slot(y, -1), "req": req},
        {"tp": token_slot(1 - y, 0), "req": req},
    )
    far, right, left, twin = (
        {"tp": tp, "req": weight_slot(1 - high, 0, core)},
        {"tp": tp, "req": weight_slot(high, 1, core)},
        {"tp": tp, "req": weight_slot(high, -1, core)},
        {"tp": tp, "req": weight_slot(high, 0, 1 - core)},
    )
    peers = (up, down, across, far, right, left, twin)

    barrier = pltpu.get_barrier_semaphore()
    for peer in peers:
        pl.semaphore_signal(barrier, inc=1, device_id=peer, device_id_type=MESH)
    pl.semaphore_wait(barrier, len(peers))

    copies = {}

    def push(name, src, dst, peer):
        index = len(copies)
        copies[name] = pltpu.make_async_remote_copy(
            src_ref=src,
            dst_ref=dst,
            send_sem=send_sem.at[index],
            recv_sem=recv_sem.at[index],
            device_id=peer,
            device_id_type=MESH,
        )
        copies[name].start()

    arrived = set()

    def await_one(name):
        copies[name].wait_recv()
        arrived.add(name)

    half = tok_ref.shape[1] // 2

    def send_token(name, part, slot, peer, own=False):
        cols = pl.ds(part * half, half)
        dst = toks.at[slot, :, cols]
        push((name, part), tok_ref.at[:, cols] if own else dst, dst, peer)

    rows = wq_ref.shape[0]

    def send_weight(name, slot, peer, own=False, part=None):
        span = pl.ds(0, rows) if part is None else pl.ds(part * (rows // 2), rows // 2)
        for tag, ref, out in (("q", wq_ref, wqs), ("o", wo_ref, wos)):
            dst = out.at[slot, span, :]
            push((name, tag), ref if own else dst, dst, peer)

    def await_weight(name):
        await_one((name, "q"))
        await_one((name, "o"))

    own_slot = token_slot(y, 0)
    own_weight = weight_slot(high, 0, core)
    for part in range(2):
        send_token("up0", part, own_slot, up, own=True)
        send_token("down0", part, own_slot, down, own=True)
        send_token("across0", part, own_slot, across, own=True)
    send_weight("right0", own_weight, right, own=True)
    send_weight("left0", own_weight, left, own=True)
    send_weight("far0", own_weight, far, own=True)
    send_weight("twin0", own_weight, twin, own=True)
    locals_ = [
        pltpu.make_async_copy(tok_ref, toks.at[own_slot], local_sem.at[0]),
        pltpu.make_async_copy(wq_ref, wqs.at[own_weight], local_sem.at[1]),
        pltpu.make_async_copy(wo_ref, wos.at[own_weight], local_sem.at[2]),
    ]
    for copy in locals_:
        copy.start()

    for part in range(2):
        await_one(("up0", part))
        send_token("up1", part, token_slot(y, -1), up)
        await_one(("down0", part))
        send_token("down1", part, token_slot(y, 1), down)
        await_one(("across0", part))
        send_token("pair_up0", part, token_slot(1 - y, 0), up)
        send_token("pair_down0", part, token_slot(1 - y, 0), down)

    await_weight("right0")
    send_weight("right1", weight_slot(high, -1, core), right, part=0)
    send_weight("twin1", weight_slot(high, -1, core), twin)
    await_weight("left0")
    send_weight("left1", weight_slot(high, 1, core), left, part=1)
    send_weight("twin2", weight_slot(high, 1, core), twin)
    await_weight("far0")
    send_weight("far_right0", weight_slot(1 - high, 0, core), right)
    send_weight("far_left0", weight_slot(1 - high, 0, core), left)
    send_weight("twin3", weight_slot(1 - high, 0, core), twin)

    for part in range(2):
        await_one(("up1", part))
        send_token("up2", part, token_slot(y, -2), up)
        send_token("across1", part, token_slot(y, -2), across)
        await_one(("down1", part))
        send_token("down2", part, token_slot(y, 2), down)
        await_one(("pair_down0", part))
        send_token("pair_down1", part, token_slot(1 - y, 1), down)

    await_weight("right1")
    await_weight("left1")
    send_weight("twin4", weight_slot(high, 2, core), twin)
    await_weight("far_right0")
    send_weight("far_right1", weight_slot(1 - high, -1, core), right, part=0)
    send_weight("twin5", weight_slot(1 - high, -1, core), twin)
    await_weight("far_left0")
    send_weight("far_left1", weight_slot(1 - high, 1, core), left, part=1)
    send_weight("twin6", weight_slot(1 - high, 1, core), twin)

    for part in range(2):
        await_one(("up2", part))
        send_token("up3", part, token_slot(y, -3), up)
        send_token("across2", part, token_slot(y, -3), across)
        await_one(("down2", part))
        send_token("across3", part, token_slot(y, 3), across)

    await_weight("far_right1")
    await_weight("far_left1")
    send_weight("twin7", weight_slot(1 - high, 2, core), twin)

    for part in range(2):
        await_one(("up3", part))
        send_token("across4", part, token_slot(y, -4), across)

    for name in copies:
        if name not in arrived:
            copies[name].wait_recv()
    for name in copies:
        copies[name].wait_send()
    for copy in locals_:
        copy.wait()


def gather_all(tokens, qkv_rows, out_rows, n_tp, n_req):
    vmem = pl.BlockSpec(memory_space=pltpu.VMEM)
    hbm = pl.BlockSpec(memory_space=pl.ANY)
    copies = 30 + 34
    return pl.pallas_call(
        functools.partial(gather_kernel, n_tp // 2, n_req // 4),
        out_shape=[
            jax.ShapeDtypeStruct((n_tp,) + tokens.shape, tokens.dtype),
            jax.ShapeDtypeStruct((n_req,) + qkv_rows.shape, qkv_rows.dtype),
            jax.ShapeDtypeStruct((n_req,) + out_rows.shape, out_rows.dtype),
        ],
        in_specs=[vmem] * 3,
        out_specs=[hbm] * 3,
        scratch_shapes=[
            pltpu.SemaphoreType.DMA((copies,)),
            pltpu.SemaphoreType.DMA((copies,)),
            pltpu.SemaphoreType.DMA((3,)),
        ],
        compiler_params=pltpu.CompilerParams(collective_id=1, has_side_effects=True),
        name="gather_all",
    )(tokens, qkv_rows, out_rows)


def body(
    tokens,
    qkv_weight,
    out_weight,
    query_key_gain,
    post_gain,
    pool_cache,
    lengths,
    prefix_pages,
    pool_order,
    owners,
):
    n_req = lax.axis_size("req")
    n_tp = lax.axis_size("tp")
    local_rows = qkv_weight.shape[0]
    local_width = qkv_weight.shape[2]
    qkv_width = 3 * local_width
    heads_here = local_width // HEAD
    block_tokens, qkv_full, out_full = gather_all(
        tokens, qkv_weight.reshape(local_rows, qkv_width), out_weight.T, n_tp, n_req
    )
    block_tokens = block_tokens.reshape(n_tp * tokens.shape[0], tokens.shape[1])
    qkv_full = qkv_full.reshape(n_req * local_rows, qkv_width)
    out_full = out_full.reshape(n_req * local_rows, local_width)
    block_len = block_tokens.shape[0]

    lengths_row = lengths[0]
    prefix_row = prefix_pages[0]
    request_of, positions, starts_at = token_layout(lengths_row, prefix_row, block_len)
    half_dim = HEAD // 2
    frequency = rope_base ** (-(2.0 * jnp.arange(half_dim, dtype=jnp.float32)) / HEAD)
    angles = positions.astype(jnp.float32)[:, None] * frequency[None, :]
    cosine = jnp.cos(angles)[:, None, :]
    sine_part = jnp.sin(angles)[:, None, :]

    pool_count = pool_cache.shape[0]
    page_ends = jnp.cumsum(prefix_row)
    page_starts = page_ends - prefix_row
    page_ids = jnp.arange(pool_count, dtype=jnp.int32)
    page_request = jnp.sum((page_ids[:, None] >= page_ends[None, :]).astype(jnp.int32), axis=1)
    key_req = jnp.repeat(page_request, PAGE)[None, :]
    pool_keys = pool_cache[:, :, 0, :].reshape(pool_count * PAGE, local_width)
    pool_values = pool_cache[:, :, 1, :].reshape(pool_count * PAGE, local_width)
    tiles = block_len // QTILE
    first_req = request_of.reshape(tiles, QTILE)[:, 0]
    last_req = request_of.reshape(tiles, QTILE)[:, -1]
    req_ids = jnp.arange(lengths_row.shape[0], dtype=jnp.int32)
    low = jnp.sum(jnp.where(first_req[:, None] == req_ids[None, :], page_starts[None, :], 0), axis=1)
    high = jnp.sum(jnp.where(last_req[:, None] == req_ids[None, :], page_ends[None, :], 0), axis=1)
    per_chunk = CHUNK // PAGE
    bounds = jnp.stack([low // per_chunk, (high + per_chunk - 1) // per_chunk]).astype(jnp.int32)

    joined_all = jnp.dot(block_tokens, qkv_full, preferred_element_type=jnp.float32)
    queries = joined_all[:, :local_width]
    keys_raw = joined_all[:, local_width : 2 * local_width]
    values_raw = joined_all[:, 2 * local_width :]
    local_sums = jnp.stack(
        [jnp.sum(queries * queries, axis=1), jnp.sum(keys_raw * keys_raw, axis=1)]
    )
    global_sums = sum_over_tp(local_sums, n_tp)
    inverse = lax.rsqrt(global_sums / (HEADS * HEAD) + norm_eps)
    queries = queries * inverse[0][:, None] * query_key_gain[0]
    keys_raw = keys_raw * inverse[1][:, None] * query_key_gain[1]
    query_rot = (
        rotate_heads(queries.reshape(block_len, heads_here, HEAD), cosine, sine_part)
        .astype(jnp.bfloat16)
        .reshape(block_len, local_width)
    )
    key_rot = (
        rotate_heads(keys_raw.reshape(block_len, heads_here, HEAD), cosine, sine_part)
        .astype(jnp.bfloat16)
        .reshape(block_len, local_width)
    )
    value_new = values_raw.astype(jnp.bfloat16)

    page_span = CAP * PAGE
    half = n_req // 2
    my_half = lax.axis_index("req") // half
    across = [(r, (r + half) % n_req) for r in range(n_req)]
    kv_new = jnp.concatenate([key_rot, value_new], axis=1)
    kv_new, query_rot = lax.optimization_barrier((kv_new, query_rot))
    kv_far = lax.ppermute(kv_new, "req", across)
    table = jnp.stack([starts_at, lengths_row, owners[0]])
    table_far = lax.ppermute(table, "req", across)
    attention = attend(
        bounds,
        pool_order,
        query_rot,
        key_rot,
        value_new,
        pool_keys,
        pool_values,
        request_of[:, None],
        request_of[None, :],
        key_req,
    )
    attention, kv_far, table_far = lax.optimization_barrier((attention, kv_far, table_far))
    offsets = jnp.arange(page_span, dtype=jnp.int32)
    token_ids = jnp.arange(block_len, dtype=jnp.int32)
    here = my_half * half + jnp.arange(half, dtype=jnp.int32)

    def take_rows(rows, starts, sizes, owner_row):
        owner_pick = (owner_row[None, :] == here[:, None]).astype(jnp.int32)
        start_of = jnp.sum(owner_pick * starts[None, :], axis=1)
        length_of = jnp.sum(owner_pick * sizes[None, :], axis=1)
        source = jnp.where(
            offsets[None, :] < length_of[:, None], start_of[:, None] + offsets[None, :], -1
        ).reshape(-1)
        select = (source[:, None] == token_ids[None, :]).astype(jnp.bfloat16)
        taken = jnp.dot(select, rows, preferred_element_type=jnp.float32).astype(jnp.bfloat16)
        return taken.reshape(half, page_span, 2 * local_width)

    near = take_rows(kv_new, table[0], table[1], table[2])
    remote = take_rows(kv_far, table_far[0], table_far[1], table_far[2])
    outgoing = jnp.stack(
        [jnp.where(my_half == 0, near, remote), jnp.where(my_half == 0, remote, near)], axis=1
    )
    arrived = lax.all_to_all(
        outgoing,
        "req",
        split_axis=0,
        concat_axis=0,
        tiled=True,
        axis_index_groups=[list(range(half)), list(range(half, n_req))],
    )
    arrived = jnp.swapaxes(arrived, 0, 1)
    handed_pages = arrived.reshape(n_req * CAP, PAGE, 2, local_width)

    partial = lax.dot_general(
        attention, out_full, (((1,), (1,)), ((), ())), preferred_element_type=jnp.float32
    ).astype(jnp.bfloat16)
    projected = lax.psum_scatter(partial, "tp", scatter_dimension=0, tiled=True).astype(jnp.float32)
    post_scale = lax.rsqrt(jnp.mean(projected * projected, axis=1, keepdims=True) + norm_eps)
    hidden = (tokens.astype(jnp.float32) + projected * post_scale * post_gain[None, :]).astype(
        jnp.bfloat16
    )
    return (hidden, handed_pages)


def solution(mesh):
    in_specs = (
        P(("req", "tp"), None),
        P("req", None, "tp"),
        P("tp", "req"),
        P(None, "tp"),
        P(),
        P("req", None, None, "tp"),
        P("req", None),
        P("req", None),
        P("req", None),
        P("req", None),
    )
    out_specs = (P(("req", "tp"), None), P("req", None, None, "tp"))
    return jax.shard_map(body, mesh=mesh, in_specs=in_specs, out_specs=out_specs, check_vma=False)
```

```python
import functools

import jax
import jax.numpy as jnp
from jax import lax
from jax.experimental import pallas as pl
from jax.experimental.pallas import tpu as pltpu
from jax.sharding import PartitionSpec as P

HEADS = 32
HEAD = 128
PAGE = 128
CAP = 2
QTILE = 128
CHUNK = 512

norm_eps = 1e-06
rope_base = 500000.0
masked_score = -1e30
log2_e = 1.4426950408889634
MESH = pl.DeviceIdType.MESH


def token_layout(lengths_row, prefix_row, block_len):
    ends_at = jnp.cumsum(lengths_row)
    starts_at = ends_at - lengths_row
    token_ids = jnp.arange(block_len, dtype=jnp.int32)
    request_of = jnp.sum((token_ids[:, None] >= ends_at[None, :]).astype(jnp.int32), axis=1)
    one_hot = (
        request_of[:, None] == jnp.arange(lengths_row.shape[0], dtype=jnp.int32)[None, :]
    ).astype(jnp.int32)
    shift_of = jnp.sum(one_hot * (prefix_row * PAGE - starts_at)[None, :], axis=1)
    return (request_of, token_ids + shift_of, starts_at)


def rotate_heads(tensor, cosine, sine_part):
    half_dim = HEAD // 2
    first_half = tensor[..., :half_dim]
    second_half = tensor[..., half_dim:]
    return jnp.concatenate(
        [
            first_half * cosine - second_half * sine_part,
            second_half * cosine + first_half * sine_part,
        ],
        axis=-1,
    )


def sum_kernel(count, x_ref, o_ref, slots, send_sem, recv_sem):
    me = lax.axis_index("tp")
    barrier = pltpu.get_barrier_semaphore()
    for d in range(1, count):
        pl.semaphore_signal(
            barrier, inc=1, device_id={"tp": lax.rem(me + d, count)}, device_id_type=MESH
        )
    pl.semaphore_wait(barrier, count - 1)
    copies = []
    for d in range(1, count):
        copy = pltpu.make_async_remote_copy(
            src_ref=x_ref,
            dst_ref=slots.at[d - 1],
            send_sem=send_sem.at[d - 1],
            recv_sem=recv_sem.at[d - 1],
            device_id={"tp": lax.rem(me + d, count)},
            device_id_type=MESH,
        )
        copy.start()
        copies.append(copy)
    for copy in copies:
        copy.wait()
    total = x_ref[...]
    for d in range(1, count):
        total = total + slots[d - 1]
    o_ref[...] = total


def sum_over_tp(x, count):
    return pl.pallas_call(
        functools.partial(sum_kernel, count),
        out_shape=jax.ShapeDtypeStruct(x.shape, x.dtype),
        in_specs=[pl.BlockSpec(memory_space=pltpu.VMEM)],
        out_specs=pl.BlockSpec(memory_space=pltpu.VMEM),
        scratch_shapes=[
            pltpu.VMEM((count - 1,) + x.shape, x.dtype),
            pltpu.SemaphoreType.DMA((count - 1,)),
            pltpu.SemaphoreType.DMA((count - 1,)),
        ],
        compiler_params=pltpu.CompilerParams(collective_id=0, has_side_effects=True),
        cost_estimate=pl.CostEstimate(flops=100000, bytes_accessed=20000000, transcendentals=0),
        name="sum_squares",
    )(x)


def attend_kernel(
    bounds_ref, order_ref, q_ref, kn_ref, vn_ref, pool_ref, row_ref, col_ref, key_ref, o_ref
):
    block_len, width = q_ref.shape
    heads_here = width // HEAD
    scale = HEAD ** (-0.5) * log2_e
    window = CAP * PAGE + QTILE

    def tile(i, _):
        r0 = pl.multiple_of(i * QTILE, QTILE)
        k0 = pl.multiple_of(jnp.maximum(i - CAP, 0) * QTILE, QTILE)
        tile_rows, tile_keys = pl.ds(r0, QTILE), pl.ds(k0, window)
        row_req = row_ref[tile_rows, :]
        row_ids = lax.broadcasted_iota(jnp.int32, (QTILE, window), 0) + r0
        col_ids = lax.broadcasted_iota(jnp.int32, (QTILE, window), 1) + k0
        block_mask = (row_req == col_ref[:, tile_keys]) & (col_ids <= row_ids)
        carry = []
        for h in range(heads_here):
            cols = slice(h * HEAD, (h + 1) * HEAD)
            scores = lax.dot_general(
                q_ref[tile_rows, cols],
                kn_ref[tile_keys, cols],
                (((1,), (1,)), ((), ())),
                preferred_element_type=jnp.float32,
            )
            scores = jnp.where(block_mask, scores * scale, masked_score)
            top = jnp.max(scores, axis=1, keepdims=True)
            weights = jnp.exp2(scores - top)
            total = jnp.sum(weights, axis=1, keepdims=True)
            mixed = jnp.dot(
                weights.astype(jnp.bfloat16), vn_ref[tile_keys, cols], preferred_element_type=jnp.float32
            )
            carry += [top, total, mixed]

        def step(j, carry):
            off = pl.multiple_of(j * CHUNK, CHUNK)
            mask = row_req == key_ref[:, pl.ds(off, CHUNK)]
            pages = [
                pl.ds(pl.multiple_of(order_ref[0, j * (CHUNK // PAGE) + e] * PAGE, PAGE), PAGE)
                for e in range(CHUNK // PAGE)
            ]
            out = []
            for h in range(heads_here):
                cols = slice(h * HEAD, (h + 1) * HEAD)
                value_cols = slice(width + h * HEAD, width + (h + 1) * HEAD)
                top, total, mixed = carry[3 * h : 3 * h + 3]
                scores = lax.dot_general(
                    q_ref[tile_rows, cols],
                    jnp.concatenate([pool_ref[page, cols] for page in pages], axis=0),
                    (((1,), (1,)), ((), ())),
                    preferred_element_type=jnp.float32,
                )
                scores = jnp.where(mask, scores * scale, masked_score)
                new_top = jnp.maximum(top, jnp.max(scores, axis=1, keepdims=True))
                fade = jnp.exp2(top - new_top)
                weights = jnp.exp2(scores - new_top)
                total = total * fade + jnp.sum(weights, axis=1, keepdims=True)
                mixed = mixed * fade + jnp.dot(
                    weights.astype(jnp.bfloat16),
                    jnp.concatenate([pool_ref[page, value_cols] for page in pages], axis=0),
                    preferred_element_type=jnp.float32,
                )
                out += [new_top, total, mixed]
            return tuple(out)

        carry = lax.fori_loop(bounds_ref[0, i], bounds_ref[1, i], step, tuple(carry))
        for h in range(heads_here):
            cols = slice(h * HEAD, (h + 1) * HEAD)
            o_ref[tile_rows, cols] = (carry[3 * h + 2] / carry[3 * h + 1]).astype(jnp.bfloat16)
        return 0

    lax.fori_loop(0, block_len // QTILE, tile, 0)


def attend(bounds, order, q, kn, vn, pool, row_req, col_req, key_req):
    vmem = pl.BlockSpec(memory_space=pltpu.VMEM)
    return pl.pallas_call(
        attend_kernel,
        out_shape=jax.ShapeDtypeStruct(q.shape, jnp.bfloat16),
        in_specs=[pl.BlockSpec(memory_space=pltpu.SMEM)] * 2 + [vmem] * 7,
        out_specs=vmem,
        cost_estimate=pl.CostEstimate(
            flops=4000000000, bytes_accessed=40000000, transcendentals=4000000
        ),
        name="paged_attention",
    )(bounds, order, q, kn, vn, pool, row_req, col_req, key_req)


def gather_kernel(
    n_z, n_x, tok_ref, wq_ref, wo_ref, toks, wqs, wos, send_sem, recv_sem, local_sem
):
    tp, req = lax.axis_index("tp"), lax.axis_index("req")
    y, z = tp // n_z, lax.rem(tp, n_z)
    high, x, core = req // (2 * n_x), lax.rem(req // 2, n_x), lax.rem(req, 2)

    def token_slot(yy, dz):
        return yy * n_z + lax.rem(z + dz + n_z, n_z)

    def weight_slot(hh, dx, cc):
        return (hh * n_x + lax.rem(x + dx + n_x, n_x)) * 2 + cc

    up, down, across = (
        {"tp": token_slot(y, 1), "req": req},
        {"tp": token_slot(y, -1), "req": req},
        {"tp": token_slot(1 - y, 0), "req": req},
    )
    far, right, left, twin = (
        {"tp": tp, "req": weight_slot(1 - high, 0, core)},
        {"tp": tp, "req": weight_slot(high, 1, core)},
        {"tp": tp, "req": weight_slot(high, -1, core)},
        {"tp": tp, "req": weight_slot(high, 0, 1 - core)},
    )
    peers = (up, down, across, far, right, left, twin)

    barrier = pltpu.get_barrier_semaphore()
    for peer in peers:
        pl.semaphore_signal(barrier, inc=1, device_id=peer, device_id_type=MESH)
    pl.semaphore_wait(barrier, len(peers))

    copies = {}

    def push(name, src, dst, peer):
        index = len(copies)
        copies[name] = pltpu.make_async_remote_copy(
            src_ref=src,
            dst_ref=dst,
            send_sem=send_sem.at[index],
            recv_sem=recv_sem.at[index],
            device_id=peer,
            device_id_type=MESH,
        )
        copies[name].start()

    arrived = set()

    def await_one(name):
        copies[name].wait_recv()
        arrived.add(name)

    half = tok_ref.shape[1] // 2

    def send_token(name, part, slot, peer, own=False):
        cols = pl.ds(part * half, half)
        dst = toks.at[slot, :, cols]
        push((name, part), tok_ref.at[:, cols] if own else dst, dst, peer)

    rows = wq_ref.shape[0]

    def send_weight(name, slot, peer, own=False, part=None):
        span = pl.ds(0, rows) if part is None else pl.ds(part * (rows // 2), rows // 2)
        for tag, ref, out in (("q", wq_ref, wqs), ("o", wo_ref, wos)):
            dst = out.at[slot, span, :]
            push((name, tag), ref if own else dst, dst, peer)

    def await_weight(name):
        await_one((name, "q"))
        await_one((name, "o"))

    own_slot = token_slot(y, 0)
    own_weight = weight_slot(high, 0, core)
    for part in range(2):
        send_token("up0", part, own_slot, up, own=True)
        send_token("down0", part, own_slot, down, own=True)
        send_token("across0", part, own_slot, across, own=True)
    send_weight("right0", own_weight, right, own=True)
    send_weight("left0", own_weight, left, own=True)
    send_weight("far0", own_weight, far, own=True)
    send_weight("twin0", own_weight, twin, own=True)
    locals_ = [
        pltpu.make_async_copy(tok_ref, toks.at[own_slot], local_sem.at[0]),
        pltpu.make_async_copy(wq_ref, wqs.at[own_weight], local_sem.at[1]),
        pltpu.make_async_copy(wo_ref, wos.at[own_weight], local_sem.at[2]),
    ]
    for copy in locals_:
        copy.start()

    for part in range(2):
        await_one(("up0", part))
        send_token("up1", part, token_slot(y, -1), up)
        await_one(("down0", part))
        send_token("down1", part, token_slot(y, 1), down)
        await_one(("across0", part))
        send_token("pair_up0", part, token_slot(1 - y, 0), up)
        send_token("pair_down0", part, token_slot(1 - y, 0), down)

    await_weight("right0")
    send_weight("right1", weight_slot(high, -1, core), right, part=0)
    send_weight("twin1", weight_slot(high, -1, core), twin)
    await_weight("left0")
    send_weight("left1", weight_slot(high, 1, core), left, part=1)
    send_weight("twin2", weight_slot(high, 1, core), twin)
    await_weight("far0")
    send_weight("far_right0", weight_slot(1 - high, 0, core), right)
    send_weight("far_left0", weight_slot(1 - high, 0, core), left)
    send_weight("twin3", weight_slot(1 - high, 0, core), twin)

    for part in range(2):
        await_one(("up1", part))
        send_token("up2", part, token_slot(y, -2), up)
        send_token("across1", part, token_slot(y, -2), across)
        await_one(("down1", part))
        send_token("down2", part, token_slot(y, 2), down)
        await_one(("pair_down0", part))
        send_token("pair_down1", part, token_slot(1 - y, 1), down)

    await_weight("right1")
    await_weight("left1")
    send_weight("twin4", weight_slot(high, 2, core), twin)
    await_weight("far_right0")
    send_weight("far_right1", weight_slot(1 - high, -1, core), right, part=0)
    send_weight("twin5", weight_slot(1 - high, -1, core), twin)
    await_weight("far_left0")
    send_weight("far_left1", weight_slot(1 - high, 1, core), left, part=1)
    send_weight("twin6", weight_slot(1 - high, 1, core), twin)

    for part in range(2):
        await_one(("up2", part))
        send_token("up3", part, token_slot(y, -3), up)
        send_token("across2", part, token_slot(y, -3), across)
        await_one(("down2", part))
        send_token("across3", part, token_slot(y, 3), across)

    await_weight("far_right1")
    await_weight("far_left1")
    send_weight("twin7", weight_slot(1 - high, 2, core), twin)

    for part in range(2):
        await_one(("up3", part))
        send_token("across4", part, token_slot(y, -4), across)

    for name in copies:
        if name not in arrived:
            copies[name].wait_recv()
    for name in copies:
        copies[name].wait_send()
    for copy in locals_:
        copy.wait()


def gather_all(tokens, qkv_rows, out_rows, n_tp, n_req):
    vmem = pl.BlockSpec(memory_space=pltpu.VMEM)
    hbm = pl.BlockSpec(memory_space=pl.ANY)
    copies = 30 + 34
    return pl.pallas_call(
        functools.partial(gather_kernel, n_tp // 2, n_req // 4),
        out_shape=[
            jax.ShapeDtypeStruct((n_tp,) + tokens.shape, tokens.dtype),
            jax.ShapeDtypeStruct((n_req,) + qkv_rows.shape, qkv_rows.dtype),
            jax.ShapeDtypeStruct((n_req,) + out_rows.shape, out_rows.dtype),
        ],
        in_specs=[vmem] * 3,
        out_specs=[hbm] * 3,
        scratch_shapes=[
            pltpu.SemaphoreType.DMA((copies,)),
            pltpu.SemaphoreType.DMA((copies,)),
            pltpu.SemaphoreType.DMA((3,)),
        ],
        compiler_params=pltpu.CompilerParams(collective_id=1, has_side_effects=True),
        name="gather_all",
    )(tokens, qkv_rows, out_rows)


def body(
    tokens,
    qkv_weight,
    out_weight,
    query_key_gain,
    post_gain,
    pool_cache,
    lengths,
    prefix_pages,
    pool_order,
    owners,
):
    n_req = lax.axis_size("req")
    n_tp = lax.axis_size("tp")
    local_rows = qkv_weight.shape[0]
    local_width = qkv_weight.shape[2]
    qkv_width = 3 * local_width
    heads_here = local_width // HEAD
    block_tokens, qkv_full, out_full = gather_all(
        tokens, qkv_weight.reshape(local_rows, qkv_width), out_weight.T, n_tp, n_req
    )
    block_tokens = block_tokens.reshape(n_tp * tokens.shape[0], tokens.shape[1])
    qkv_full = qkv_full.reshape(n_req * local_rows, qkv_width)
    out_full = out_full.reshape(n_req * local_rows, local_width)
    block_len = block_tokens.shape[0]

    lengths_row = lengths[0]
    prefix_row = prefix_pages[0]
    request_of, positions, starts_at = token_layout(lengths_row, prefix_row, block_len)
    half_dim = HEAD // 2
    frequency = rope_base ** (-(2.0 * jnp.arange(half_dim, dtype=jnp.float32)) / HEAD)
    angles = positions.astype(jnp.float32)[:, None] * frequency[None, :]
    cosine = jnp.cos(angles)[:, None, :]
    sine_part = jnp.sin(angles)[:, None, :]

    pool_count = pool_cache.shape[0]
    page_ends = jnp.cumsum(prefix_row)
    page_starts = page_ends - prefix_row
    page_ids = jnp.arange(pool_count, dtype=jnp.int32)
    page_request = jnp.sum((page_ids[:, None] >= page_ends[None, :]).astype(jnp.int32), axis=1)
    key_req = jnp.repeat(page_request, PAGE)[None, :]
    pool_rows = pool_cache.reshape(pool_count * PAGE, 2 * local_width)
    tiles = block_len // QTILE
    first_req = request_of.reshape(tiles, QTILE)[:, 0]
    last_req = request_of.reshape(tiles, QTILE)[:, -1]
    req_ids = jnp.arange(lengths_row.shape[0], dtype=jnp.int32)
    low = jnp.sum(jnp.where(first_req[:, None] == req_ids[None, :], page_starts[None, :], 0), axis=1)
    high = jnp.sum(jnp.where(last_req[:, None] == req_ids[None, :], page_ends[None, :], 0), axis=1)
    per_chunk = CHUNK // PAGE
    bounds = jnp.stack([low // per_chunk, (high + per_chunk - 1) // per_chunk]).astype(jnp.int32)

    joined_all = jnp.dot(block_tokens, qkv_full, preferred_element_type=jnp.float32)
    queries = joined_all[:, :local_width]
    keys_raw = joined_all[:, local_width : 2 * local_width]
    values_raw = joined_all[:, 2 * local_width :]
    local_sums = jnp.stack(
        [jnp.sum(queries * queries, axis=1), jnp.sum(keys_raw * keys_raw, axis=1)]
    )
    global_sums = sum_over_tp(local_sums, n_tp)
    inverse = lax.rsqrt(global_sums / (HEADS * HEAD) + norm_eps)
    queries = queries * inverse[0][:, None] * query_key_gain[0]
    keys_raw = keys_raw * inverse[1][:, None] * query_key_gain[1]
    query_rot = (
        rotate_heads(queries.reshape(block_len, heads_here, HEAD), cosine, sine_part)
        .astype(jnp.bfloat16)
        .reshape(block_len, local_width)
    )
    key_rot = (
        rotate_heads(keys_raw.reshape(block_len, heads_here, HEAD), cosine, sine_part)
        .astype(jnp.bfloat16)
        .reshape(block_len, local_width)
    )
    value_new = values_raw.astype(jnp.bfloat16)

    page_span = CAP * PAGE
    half = n_req // 2
    my_half = lax.axis_index("req") // half
    across = [(r, (r + half) % n_req) for r in range(n_req)]
    kv_new = jnp.concatenate([key_rot, value_new], axis=1)
    kv_new, query_rot = lax.optimization_barrier((kv_new, query_rot))
    kv_far = lax.ppermute(kv_new, "req", across)
    table = jnp.stack([starts_at, lengths_row, owners[0]])
    table_far = lax.ppermute(table, "req", across)
    attention = attend(
        bounds,
        pool_order,
        query_rot,
        key_rot,
        value_new,
        pool_rows,
        request_of[:, None],
        request_of[None, :],
        key_req,
    )
    attention, kv_far, table_far = lax.optimization_barrier((attention, kv_far, table_far))
    offsets = jnp.arange(page_span, dtype=jnp.int32)
    token_ids = jnp.arange(block_len, dtype=jnp.int32)
    here = my_half * half + jnp.arange(half, dtype=jnp.int32)

    def take_rows(rows, starts, sizes, owner_row):
        owner_pick = (owner_row[None, :] == here[:, None]).astype(jnp.int32)
        start_of = jnp.sum(owner_pick * starts[None, :], axis=1)
        length_of = jnp.sum(owner_pick * sizes[None, :], axis=1)
        source = jnp.where(
            offsets[None, :] < length_of[:, None], start_of[:, None] + offsets[None, :], -1
        ).reshape(-1)
        select = (source[:, None] == token_ids[None, :]).astype(jnp.bfloat16)
        taken = jnp.dot(select, rows, preferred_element_type=jnp.float32).astype(jnp.bfloat16)
        return taken.reshape(half, page_span, 2 * local_width)

    near = take_rows(kv_new, table[0], table[1], table[2])
    remote = take_rows(kv_far, table_far[0], table_far[1], table_far[2])
    outgoing = jnp.stack(
        [jnp.where(my_half == 0, near, remote), jnp.where(my_half == 0, remote, near)], axis=1
    )
    arrived = lax.all_to_all(
        outgoing,
        "req",
        split_axis=0,
        concat_axis=0,
        tiled=True,
        axis_index_groups=[list(range(half)), list(range(half, n_req))],
    )
    arrived = jnp.swapaxes(arrived, 0, 1)
    handed_pages = arrived.reshape(n_req * CAP, PAGE, 2, local_width)

    partial = lax.dot_general(
        attention, out_full, (((1,), (1,)), ((), ())), preferred_element_type=jnp.float32
    ).astype(jnp.bfloat16)
    projected = lax.psum_scatter(partial, "tp", scatter_dimension=0, tiled=True).astype(jnp.float32)
    post_scale = lax.rsqrt(jnp.mean(projected * projected, axis=1, keepdims=True) + norm_eps)
    hidden = (tokens.astype(jnp.float32) + projected * post_scale * post_gain[None, :]).astype(
        jnp.bfloat16
    )
    return (hidden, handed_pages)


def solution(mesh):
    in_specs = (
        P(("req", "tp"), None),
        P("req", None, "tp"),
        P("tp", "req"),
        P(None, "tp"),
        P(),
        P("req", None, None, "tp"),
        P("req", None),
        P("req", None),
        P("req", None),
        P("req", None),
    )
    out_specs = (P(("req", "tp"), None), P("req", None, None, "tp"))
    return jax.shard_map(body, mesh=mesh, in_specs=in_specs, out_specs=out_specs, check_vma=False)
```
